512 devices in a mesh: sec: 16 (over z_hi, y), term: 32 (over z_lo, x, core).
Axes of the slice: x: 4, y: 8, z: 8 (z_hi: 2, z_lo: 4; z = z_hi * 4 + z_lo), core: 2. Of those that a mesh axis runs over, the one named last changes fastest.
Arguments:
- psi: bfloat16 [32, 2, 512, 512], P('sec'), may hold values from -6 to 6
- left_ops: bfloat16 [32, 32, 512, 512], P('term', 'sec'), may hold values from -0.25 to 0.25
- right_ops: bfloat16 [32, 32, 512, 512], P('term', 'sec'), may hold values from -0.046875 to 0.046875
- shift: int32 [32], P('term'), may hold values from -2 to 2, as said below
- live: int32 [32], P('term'), may hold values 0 or 1
Outputs:
- sigma: bfloat16 [32, 2, 512, 512], P('sec', None, 'term')
The draws below stay inside these ranges and needn't reach their ends.
Inputs may be any that keep to these rules, and one draw needn't show every extreme that they name: `shift`: every draw holds both -2 and 2.
All inputs are finite; a program needn't handle non-finite values. No bound on the sum of `live` on one device may be relied on, other than what follows from the above.
Results may differ from the reference program's by a relative error of at most 0.0049.
Values may be sent and summed in bfloat16 or wider, within the bound.
A program may use at most 64 MiB of HBM per device.

```python
import jax
import jax.numpy as jnp
from jax import lax

B = 512
V = 2
DQ = 2
NSEC = 32
TERMS = 32


def draw_shift(key, part):
    values = jax.random.randint(key, (TERMS,), -DQ, DQ + 1, dtype=jnp.int32)
    return values.at[0].set(-DQ).at[1].set(DQ)


def touch_ends(result, own_key, least, high):
    longest = result.shape.index(max(result.shape))
    spots = []
    for shift in (0, 1):
        where = [jax.random.randint(jax.random.fold_in(own_key, axis), (), 0, length) for axis, length in enumerate(result.shape)]
        where[longest] = (where[longest] + shift) % result.shape[longest]
        spots.append(tuple(where))
    return result.at[spots[0]].set(least).at[spots[1]].set(high)


def block_levels(stream_key, extent, shards, low, high):
    factor_of = 1.0
    for position, blocks in shards:
        draws = jax.random.uniform(jax.random.fold_in(jax.random.fold_in(stream_key, 6), position), (blocks,), jnp.float32, low / len(shards), high / len(shards))
        factor_of = factor_of * jnp.repeat(jnp.exp(draws), extent[position] // blocks).reshape((-1,) + (1,) * (len(extent) - 1 - position))
    return factor_of


def gaussian(stream_key, extent, deviation, most, shards=(), kind=jnp.bfloat16):
    factor_of = block_levels(stream_key, extent, shards, -0.22, 0.18) if shards else 1.0
    entries = jax.random.normal(stream_key, extent, jnp.float32) * deviation * factor_of
    return jnp.minimum(jnp.maximum(entries, -most), most).astype(kind)


def setup_inputs(seed: int = 0) -> dict:
    splits = jax.random.split(jax.random.key(seed), 6)
    return {
        "psi": gaussian(splits[0], (NSEC, V, B, B), 1.0, 6.0, ((0, 16),)),
        "left_ops": gaussian(splits[1], (TERMS, NSEC, B, B), B ** -0.5, 0.25, ((0, 32), (1, 16))),
        "right_ops": gaussian(splits[2], (TERMS, NSEC, B, B), (B * TERMS) ** -0.5, 0.046875, ((0, 32), (1, 16))),
        "shift": draw_shift(jax.random.fold_in(splits[5], 71), 0),
        "live": touch_ends((jax.random.randint(splits[4], (TERMS,), 0, 4) < 3).astype(jnp.int32), jax.random.fold_in(splits[4], 1), 0, 1),
    }


def reference(psi, left_ops, right_ops, shift, live):
    padded = jnp.pad(psi, ((DQ, DQ), (0, 0), (0, 0), (0, 0)))

    def one_term(acc, index):
        start = (DQ - shift[index]).astype(jnp.int32)
        block = lax.dynamic_slice_in_dim(padded, start, NSEC, 0)
        inner = jnp.einsum('sab,svbc->svac', left_ops[index].astype(jnp.float32), block.astype(jnp.float32)).astype(jnp.bfloat16)
        outer = jnp.einsum('svac,sdc->svad', inner.astype(jnp.float32), right_ops[index].astype(jnp.float32))
        return acc + outer * live[index].astype(jnp.float32), None

    start_acc = jnp.zeros((NSEC, V, B, B), jnp.float32)
    total, _ = lax.scan(one_term, start_acc, jnp.arange(TERMS, dtype=jnp.int32))
    return total.astype(jnp.bfloat16)
```

```python
import jax
import jax.numpy as jnp
from jax import lax
from jax.experimental import pallas as pl
from jax.experimental.pallas import tpu as pltpu
from jax.sharding import PartitionSpec as P

B = 512
V = 2
NX = 4
NZ = 4
RB = 16
CUT = 8
LAST = 15
MESH = pl.DeviceIdType.MESH
f32 = jnp.float32
bf16 = jnp.bfloat16


def kernel(
    shift_ref, live_ref, psi, left, right, out,
    lbuf, rbuf, win0, win1, acc0, acc1, cex0, cex1, pair0, pair1,
    xin0, xin1, xsum0, xsum1, zin0, zin1,
    load_sem, ysend, yrecv, esend, erecv, qsend, qrecv, fsend, frecv,
    csend, crecv, xsend, xrecv, zsend, zrecv,
):
    wins, accs, cexs, pairs = (win0, win1), (acc0, acc1), (cex0, cex1), (pair0, pair1)
    xins, xsums, zins = (xin0, xin1), (xsum0, xsum1), (zin0, zin1)
    sec, term = lax.axis_index("sec"), lax.axis_index("term")
    core = lax.rem(term, 2)
    chip = term // 2
    x = lax.rem(chip, NX)
    z = chip // NX

    def dev(s, zz, xx, cc):
        return (s, (zz * NX + xx) * 2 + cc)

    sibling = dev(sec, z, x, 1 - core)
    xpeer = [dev(sec, z, lax.rem(x + k, NX), core) for k in (1, 2, 3)]
    zpeer = [dev(sec, lax.rem(z + k, NZ), x, core) for k in (1, 2, 3)]
    has_low, has_high = sec > 0, sec < LAST
    cross_low, cross_high = sec == CUT, sec == CUT - 1
    low = dev(sec - 1, jnp.where(cross_low, NZ - 1 - z, z), x, core)
    high = dev(sec + 1, jnp.where(cross_high, NZ - 1 - z, z), x, core)

    loads = [
        pltpu.make_async_copy(psi.at[:, 0], win0.at[pl.ds(2, 2)], load_sem.at[0]),
        pltpu.make_async_copy(psi.at[:, 1], win1.at[pl.ds(2, 2)], load_sem.at[1]),
        pltpu.make_async_copy(left.at[0], lbuf, load_sem.at[2]),
        pltpu.make_async_copy(right.at[0], rbuf, load_sem.at[3]),
    ]
    for copy in loads:
        copy.start()

    barrier = pltpu.get_barrier_semaphore()
    for peer in [sibling] + xpeer + zpeer:
        pl.semaphore_signal(barrier, inc=1, device_id=peer, device_id_type=MESH)

    @pl.when(has_low)
    def _():
        pl.semaphore_signal(barrier, inc=1, device_id=low, device_id_type=MESH)

    @pl.when(has_high)
    def _():
        pl.semaphore_signal(barrier, inc=1, device_id=high, device_id_type=MESH)

    ends = jnp.where(has_low, 1, 0) + jnp.where(has_high, 1, 0)
    pl.semaphore_wait(barrier, 7 + ends)

    rows = pl.ds(pl.multiple_of(x * (B // NX), B // NX), B // NX)

    has = (has_low, has_high)
    cross = (cross_low, cross_high)
    direct = tuple(jnp.logical_and(h, jnp.logical_not(c)) for h, c in zip(has, cross))
    peer_of = (low, high)

    def remote(src, dst, ssem, rsem, device):
        return pltpu.make_async_remote_copy(
            src_ref=src, dst_ref=dst, send_sem=ssem, recv_sem=rsem, device_id=device, device_id_type=MESH
        )

    def halo_send(v, side):
        at = core + 4 * (1 - side)
        return remote(psi.at[core, v], wins[v].at[at], ysend.at[v, side], yrecv.at[v, 1 - side], peer_of[side])

    def entry_send(v, side):
        at = core + 4 * (1 - side)
        return remote(
            psi.at[core, v, rows], wins[v].at[at, rows], esend.at[v, side], erecv.at[v, 1 - side], peer_of[side]
        )

    def halo_recv(v, side):
        at = core + 4 * side
        return remote(psi.at[core, v], wins[v].at[at], ysend.at[v, side], yrecv.at[v, side], peer_of[side])

    def entry_recv(v, side):
        at = core + 4 * side
        return remote(
            psi.at[core, v, rows], wins[v].at[at, rows], esend.at[v, side], erecv.at[v, side], peer_of[side]
        )

    def quarter(v, side, k):
        at = core + 4 * side
        return remote(
            wins[v].at[at, rows], wins[v].at[at, rows], qsend.at[v, side, k], qrecv.at[v, side, k], xpeer[k]
        )

    def quarter_in(v, side, k):
        at = core + 4 * side
        whose = lax.rem(x + NX - 1 - k, NX)
        theirs = pl.ds(pl.multiple_of(whose * (B // NX), B // NX), B // NX)
        return remote(
            wins[v].at[at, theirs], wins[v].at[at, theirs], qsend.at[v, side, k], qrecv.at[v, side, k], xpeer[k]
        )

    def forward(v, side):
        at = core + 4 * side
        return remote(wins[v].at[at], wins[v].at[at], fsend.at[v, side], frecv.at[v, side], sibling)

    def forward_in(v, side):
        at = 1 - core + 4 * side
        return remote(wins[v].at[at], wins[v].at[at], fsend.at[v, side], frecv.at[v, side], sibling)

    def start_halo(v):
        for side in (0, 1):
            @pl.when(direct[side])
            def _():
                halo_send(v, side).start()

            @pl.when(cross[side])
            def _():
                entry_send(v, side).start()

    def sent_halo(v):
        for side in (0, 1):
            @pl.when(direct[side])
            def _():
                halo_send(v, side).wait_send()

            @pl.when(cross[side])
            def _():
                entry_send(v, side).wait_send()

    def pass_halo(v):
        for side in (0, 1):
            @pl.when(cross[side])
            def _():
                entry_recv(v, side).wait_recv()
                for k in range(3):
                    quarter(v, side, k).start()

        for side in (0, 1):
            @pl.when(direct[side])
            def _():
                halo_recv(v, side).wait_recv()
                forward(v, side).start()

        for side in (0, 1):
            @pl.when(cross[side])
            def _():
                for k in range(3):
                    quarter_in(v, side, k).wait_recv()
                forward(v, side).start()

    def finish_halo(v):
        for side in (0, 1):
            @pl.when(has[side])
            def _():
                forward_in(v, side).wait_recv()

    def drain_halo(v):
        for side in (0, 1):
            @pl.when(has[side])
            def _():
                forward(v, side).wait_send()

            @pl.when(cross[side])
            def _():
                for k in range(3):
                    quarter(v, side, k).wait_send()

    def exchange(v, s):
        return remote(
            accs[v].at[s, :, 1 - core], cexs[v].at[s], csend.at[v, s], crecv.at[v, s], sibling
        )

    def xsend_of(v, s, k):
        return remote(
            pairs[v].at[s, :, lax.rem(x + 1 + k, NX)], xins[v].at[s, k],
            xsend.at[v, s, k], xrecv.at[v, s, k], xpeer[k],
        )

    def zsend_of(v, s, k):
        return remote(
            xsums[v].at[s, lax.rem(z + 1 + k, NZ)], zins[v].at[s, k],
            zsend.at[v, s, k], zrecv.at[v, s, k], zpeer[k],
        )

    def compute(v, s):
        block = wins[v][s + 2 - shift_ref[0]]
        inner = jnp.dot(lbuf[s], block, preferred_element_type=f32).astype(bf16)
        outer = lax.dot_general(inner, rbuf[s], (((1,), (1,)), ((), ())), preferred_element_type=f32)
        outer = outer * live_ref[0].astype(f32)
        accs[v][s] = outer.astype(bf16).reshape(NX * NZ, 2, RB, B)

    start_halo(0)
    for side in (0, 1):
        @pl.when(jnp.logical_not(has[side]))
        def _():
            for v in range(V):
                for at in range(2):
                    wins[v][4 * side + at] = jnp.zeros((B, B), bf16)

    for copy in loads:
        copy.wait()

    for v in range(V):
        pass_halo(v)
        sent_halo(v)
        if v + 1 < V:
            start_halo(v + 1)
        finish_halo(v)
        for s in range(2):
            compute(v, s)
            exchange(v, s).start()
        for s in range(2):
            exchange(v, s).wait_recv()
            both = accs[v][s, :, core].astype(f32) + cexs[v][s].astype(f32)
            pairs[v][s] = both.astype(bf16).reshape(NZ, NX, RB, B)
            for k in range(3):
                xsend_of(v, s, k).start()
        for s in range(2):
            total = pairs[v][s, :, x].astype(f32)
            for k in range(3):
                xsend_of(v, s, k).wait_recv()
                total += xins[v][s, k].astype(f32)
            xsums[v][s] = total.astype(bf16)
            for k in range(3):
                zsend_of(v, s, k).start()
        for s in range(2):
            total = xsums[v][s, z].astype(f32)
            for k in range(3):
                zsend_of(v, s, k).wait_recv()
                total += zins[v][s, k].astype(f32)
            out[s, v] = total.astype(bf16)

    for v in range(V):
        drain_halo(v)
        for s in range(2):
            exchange(v, s).wait_send()
            for k in range(3):
                xsend_of(v, s, k).wait_send()
                zsend_of(v, s, k).wait_send()


def local(psi, left_ops, right_ops, shift, live):
    dma = pltpu.SemaphoreType.DMA
    pairs_of = lambda shape: [pltpu.VMEM(shape, bf16)] * V
    hbm = pl.BlockSpec(memory_space=pl.ANY)
    smem = pl.BlockSpec(memory_space=pltpu.SMEM)
    return pl.pallas_call(
        kernel,
        out_shape=jax.ShapeDtypeStruct((2, V, RB, B), bf16),
        in_specs=[smem, smem, hbm, hbm, hbm],
        out_specs=pl.BlockSpec(memory_space=pltpu.VMEM),
        scratch_shapes=[pltpu.VMEM((2, B, B), bf16)] * 2
        + pairs_of((6, B, B))
        + pairs_of((2, NX * NZ, 2, RB, B))
        + pairs_of((2, NX * NZ, RB, B))
        + pairs_of((2, NZ, NX, RB, B))
        + pairs_of((2, 3, NZ, RB, B))
        + pairs_of((2, NZ, RB, B))
        + pairs_of((2, 3, RB, B))
        + [dma((4,))]
        + [dma((V, 2))] * 4
        + [dma((V, 2, 3))] * 2
        + [dma((V, 2))] * 2
        + [dma((V, 2))] * 2
        + [dma((V, 2, 3))] * 4,
        compiler_params=pltpu.CompilerParams(
            collective_id=0, has_side_effects=True, vmem_limit_bytes=40 * 2**20
        ),
        name="sigma",
    )(shift, live, psi, left_ops, right_ops)


def solution(mesh):
    in_specs = (
        P("sec", None, None, None),
        P("term", "sec", None, None),
        P("term", "sec", None, None),
        P("term"),
        P("term"),
    )
    out_specs = P("sec", None, "term", None)
    return jax.shard_map(local, mesh=mesh, in_specs=in_specs, out_specs=out_specs, check_vma=False)
```

```python
import jax
import jax.numpy as jnp
from jax import lax
from jax.experimental import pallas as pl
from jax.experimental.pallas import tpu as pltpu
from jax.sharding import PartitionSpec as P

B = 512
V = 2
NX = 4
NZ = 4
RB = 16
QR = B // NX
NF = 192
HF = NF // 2
ND = B - 2 * NF
VMEM_LIMIT = 60 * 2**20
CUT = 8
LAST = 15
MESH = pl.DeviceIdType.MESH
HALO, COMP, RS = 1, 1, 3
f32 = jnp.float32
bf16 = jnp.bfloat16


def kernel(
    shift_ref, live_ref, psi, left, right, out,
    lbuf, rbuf, win0, win1, acc0, acc1, cex0, cex1, pair0, pair1,
    xin0, xin1, xsum0, xsum1, zin0, zin1,
    load_sem, ysend, yrecv, hsend, hrecv, esend, erecv, qsend, qrecv,
    fsend, frecv, csend, crecv, xsend, xrecv, zsend, zrecv,
):
    wins, accs, cexs, pairs = (win0, win1), (acc0, acc1), (cex0, cex1), (pair0, pair1)
    xins, xsums, zins = (xin0, xin1), (xsum0, xsum1), (zin0, zin1)
    sec, term = lax.axis_index("sec"), lax.axis_index("term")
    core = lax.rem(term, 2)
    chip = term // 2
    x = lax.rem(chip, NX)
    z = chip // NX
    xa = (lax.rem(x + NX - 1, NX), lax.rem(x + 1, NX))

    def dev(s, zz, xx, cc):
        return (s, (zz * NX + xx) * 2 + cc)

    sibling = dev(sec, z, x, 1 - core)
    xpeer = [dev(sec, z, xx, core) for xx in xa]
    xring = [dev(sec, z, lax.rem(x + k, NX), core) for k in (1, 2, 3)]
    zpeer = [dev(sec, lax.rem(z + k, NZ), x, core) for k in (1, 2, 3)]
    has = (sec > 0, sec < LAST)
    cross = (sec == CUT, sec == CUT - 1)
    direct = tuple(jnp.logical_and(h, jnp.logical_not(c)) for h, c in zip(has, cross))
    ypeer = (
        dev(sec - 1, jnp.where(cross[0], NZ - 1 - z, z), x, core),
        dev(sec + 1, jnp.where(cross[1], NZ - 1 - z, z), x, core),
    )

    loads = [
        pltpu.make_async_copy(psi.at[:, 0], win0.at[pl.ds(2, 2)], load_sem.at[0]),
        pltpu.make_async_copy(psi.at[:, 1], win1.at[pl.ds(2, 2)], load_sem.at[1]),
        pltpu.make_async_copy(left.at[0], lbuf, load_sem.at[2]),
        pltpu.make_async_copy(right.at[0], rbuf, load_sem.at[3]),
    ]
    for copy in loads:
        copy.start()

    barrier = pltpu.get_barrier_semaphore()
    for peer in [sibling] + xring + zpeer:
        pl.semaphore_signal(barrier, inc=1, device_id=peer, device_id_type=MESH)
    for side in (0, 1):
        @pl.when(has[side])
        def _():
            pl.semaphore_signal(barrier, inc=1, device_id=ypeer[side], device_id_type=MESH)

    ends = jnp.where(has[0], 1, 0) + jnp.where(has[1], 1, 0)
    pl.semaphore_wait(barrier, 7 + ends)

    def remote(src, dst, ssem, rsem, device):
        return pltpu.make_async_remote_copy(
            src_ref=src, dst_ref=dst, send_sem=ssem, recv_sem=rsem, device_id=device, device_id_type=MESH
        )

    odd = lax.rem(x, 2)

    def block_rows(n):
        return pl.ds(pl.multiple_of(n * QR, QR), QR)

    def shared_rows(parity, q):
        return pl.ds(pl.multiple_of(parity * NF + q * HF, HF), HF)

    def y_rows(side, j):
        return pl.ds(2 * NF, ND) if j == 2 else shared_rows(odd, j ^ side)

    def spot(side):
        return core + 4 * side

    def y_copy(v, side, j, landing):
        at = side if landing else 1 - side
        part = y_rows(at, j)
        return remote(
            psi.at[core, v, part], wins[v].at[spot(at), part], ysend.at[v, side, j], yrecv.at[v, at, j], ypeer[side]
        )

    def h_copy(v, side, q, landing):
        part = shared_rows(1 - odd, q) if landing else shared_rows(odd, q)
        place = wins[v].at[spot(side), part]
        return remote(place, place, hsend.at[v, side, q], hrecv.at[v, side, q], xpeer[q])

    def e_copy(v, side, landing):
        at = side if landing else 1 - side
        part = block_rows(x)
        return remote(
            psi.at[core, v, part], wins[v].at[spot(at), part], esend.at[v, side], erecv.at[v, at], ypeer[side]
        )

    def q_copy(v, side, k, landing):
        place = wins[v].at[spot(side), block_rows(lax.rem(x + 3 - k, NX) if landing else x)]
        return remote(place, place, qsend.at[v, side, k], qrecv.at[v, side, k], xring[k])

    def pass_on(v, side, part, n):
        place = wins[v].at[spot(side), part]
        return remote(place, place, fsend.at[v, side, n], frecv.at[v, side], sibling)

    def passed(v, side):
        place = wins[v].at[1 - core + 4 * side]
        return remote(place, place, fsend.at[v, side, 0], frecv.at[v, side], sibling)

    def issue_y(v, j):
        if j == 2 and not ND:
            return
        for side in (0, 1):
            @pl.when(direct[side])
            def _():
                y_copy(v, side, j, False).start()

    def issue_e(v):
        for side in (0, 1):
            @pl.when(cross[side])
            def _():
                e_copy(v, side, False).start()

    def pass_y(v, j):
        if j == 2 and not ND:
            return
        for side in (0, 1):
            @pl.when(direct[side])
            def _():
                y_copy(v, side, j, True).wait_recv()
                if j < 2:
                    h_copy(v, side, j ^ side, False).start()
                pass_on(v, side, y_rows(side, j), j).start()

    def pass_x(v, j):
        for side in (0, 1):
            @pl.when(direct[side])
            def _():
                h_copy(v, side, j ^ side, True).wait_recv()
                pass_on(v, side, shared_rows(1 - odd, j ^ side), 3 + j).start()

    def pass_e(v):
        for side in (0, 1):
            @pl.when(cross[side])
            def _():
                e_copy(v, side, True).wait_recv()
                for k in range(3):
                    q_copy(v, side, k, False).start()
                pass_on(v, side, block_rows(x), 0).start()

    def pass_q(v):
        for side in (0, 1):
            @pl.when(cross[side])
            def _():
                for k in (0, 2, 1):
                    q_copy(v, side, k, True).wait_recv()
                    pass_on(v, side, block_rows(lax.rem(x + 3 - k, NX)), 1 + k).start()

    def finish(v):
        for side in (0, 1):
            @pl.when(has[side])
            def _():
                passed(v, side).wait_recv()

    def drain(v):
        for side in (0, 1):
            @pl.when(direct[side])
            def _():
                for j in (0, 1, 2):
                    if j < 2 or ND:
                        y_copy(v, side, j, False).wait_send()
                        pass_on(v, side, y_rows(side, j), j).wait_send()
                for j in (0, 1):
                    h_copy(v, side, j, False).wait_send()
                    pass_on(v, side, shared_rows(0, 0), 3 + j).wait_send()

            @pl.when(cross[side])
            def _():
                e_copy(v, side, False).wait_send()
                for k in range(3):
                    q_copy(v, side, k, False).wait_send()
                for n in range(4):
                    pass_on(v, side, block_rows(0), n).wait_send()

    def exchange(v, s):
        return remote(accs[v].at[s, :, 1 - core], cexs[v].at[s], csend.at[v, s], crecv.at[v, s], sibling)

    def xhop(v, s, k):
        return remote(
            pairs[v].at[s, :, lax.rem(x + 1 + k, NX)], xins[v].at[s, k], xsend.at[v, s, k], xrecv.at[v, s, k], xring[k]
        )

    def zhop(v, s, k):
        return remote(
            xsums[v].at[s, lax.rem(z + 1 + k, NZ)], zins[v].at[s, k], zsend.at[v, s, k], zrecv.at[v, s, k], zpeer[k]
        )

    def compute(v, s):
        block = wins[v][s + 2 - shift_ref[0]]
        inner = jnp.dot(lbuf[s], block, preferred_element_type=f32).astype(bf16)
        outer = lax.dot_general(inner, rbuf[s], (((1,), (1,)), ((), ())), preferred_element_type=f32)
        outer = outer * live_ref[0].astype(f32)
        accs[v][s] = outer.astype(bf16).reshape(NX * NZ, 2, RB, B)

    def products(v):
        for s in range(2):
            if COMP:
                compute(v, s)
            if RS >= 1:
                exchange(v, s).start()

    def add_cores(v):
        for s in range(2 if RS >= 1 else 0):
            exchange(v, s).wait_recv()
            both = accs[v][s, :, core].astype(f32) + cexs[v][s].astype(f32)
            pairs[v][s] = both.astype(bf16).reshape(NZ, NX, RB, B)
            if RS >= 2:
                for k in range(3):
                    xhop(v, s, k).start()

    def add_x(v):
        for s in range(2 if RS >= 2 else 0):
            total = pairs[v][s, :, x].astype(f32)
            for k in range(3):
                xhop(v, s, k).wait_recv()
                total += xins[v][s, k].astype(f32)
            xsums[v][s] = total.astype(bf16)
            if RS >= 3:
                for k in range(3):
                    zhop(v, s, k).start()

    def add_z(v):
        for s in range(2 if RS >= 3 else 0):
            total = xsums[v][s, z].astype(f32)
            for k in range(3):
                zhop(v, s, k).wait_recv()
                total += zins[v][s, k].astype(f32)
            out[s, v] = total.astype(bf16)

    if HALO:
        issue_y(0, 0)
        issue_e(0)
        issue_y(0, 1)
    for side in (0, 1):
        @pl.when(jnp.logical_not(has[side]))
        def _():
            for v in range(V):
                for at in range(2):
                    wins[v][4 * side + at] = jnp.zeros((B, B), bf16)

    for copy in loads:
        copy.wait()

    at_cut = jnp.logical_or(cross[0], cross[1])
    if HALO:
        pass_y(0, 0)
        issue_y(0, 2)
        if not ND:
            issue_y(1, 0)
        pass_y(0, 1)
        if ND:
            issue_y(1, 0)
        else:
            issue_y(1, 1)
        pass_e(0)
        issue_e(1)
        pass_x(0, 0)
        pass_y(0, 2)
        if ND:
            issue_y(1, 1)
        pass_x(0, 1)
        pass_y(1, 0)
        issue_y(1, 2)

        @pl.when(at_cut)
        def _():
            pass_y(1, 1)
            pass_e(1)
            pass_q(0)

        finish(0)
    products(0)
    if HALO:
        @pl.when(jnp.logical_not(at_cut))
        def _():
            pass_y(1, 1)

    add_cores(0)
    if HALO:
        pass_x(1, 0)
        pass_y(1, 2)
        pass_x(1, 1)
        pass_q(1)
        finish(1)
    products(1)
    add_x(0)
    add_cores(1)
    add_z(0)
    add_x(1)
    add_z(1)

    for v in range(V):
        if HALO:
            drain(v)
        for s in range(2):
            if RS >= 1:
                exchange(v, s).wait_send()
            if RS >= 2:
                for k in range(3):
                    xhop(v, s, k).wait_send()
            if RS >= 3:
                for k in range(3):
                    zhop(v, s, k).wait_send()


def local(psi, left_ops, right_ops, shift, live):
    dma = pltpu.SemaphoreType.DMA
    per_vector = lambda shape: [pltpu.VMEM(shape, bf16)] * V
    hbm = pl.BlockSpec(memory_space=pltpu.HBM)
    smem = pl.BlockSpec(memory_space=pltpu.SMEM)
    return pl.pallas_call(
        kernel,
        out_shape=jax.ShapeDtypeStruct((2, V, RB, B), bf16),
        in_specs=[smem, smem, hbm, hbm, hbm],
        out_specs=pl.BlockSpec(memory_space=pltpu.VMEM),
        scratch_shapes=[pltpu.VMEM((2, B, B), bf16)] * 2
        + per_vector((6, B, B))
        + per_vector((2, NX * NZ, 2, RB, B))
        + per_vector((2, NX * NZ, RB, B))
        + per_vector((2, NZ, NX, RB, B))
        + per_vector((2, 3, NZ, RB, B))
        + per_vector((2, NZ, RB, B))
        + per_vector((2, 3, RB, B))
        + [dma((4,))]
        + [dma((V, 2, 3))] * 2
        + [dma((V, 2, 2))] * 2
        + [dma((V, 2))] * 2
        + [dma((V, 2, 3))] * 2
        + [dma((V, 2, 5)), dma((V, 2))]
        + [dma((V, 2))] * 2
        + [dma((V, 2, 3))] * 4,
        compiler_params=pltpu.CompilerParams(
            collective_id=0, has_side_effects=True, vmem_limit_bytes=VMEM_LIMIT
        ),
        name="sigma",
    )(shift, live, psi, left_ops, right_ops)


def solution(mesh):
    in_specs = (
        P("sec", None, None, None),
        P("term", "sec", None, None),
        P("term", "sec", None, None),
        P("term"),
        P("term"),
    )
    out_specs = P("sec", None, "term", None)
    return jax.shard_map(local, mesh=mesh, in_specs=in_specs, out_specs=out_specs, check_vma=False)
```

```python
import jax
import jax.numpy as jnp
from jax import lax
from jax.experimental import pallas as pl
from jax.experimental.pallas import tpu as pltpu
from jax.sharding import PartitionSpec as P

B = 512
V = 2
NX = 4
NZ = 4
RB = 16
QR = B // NX
QH = QR // 2
NF = 128
HF = NF // 2
ND = B - 2 * NF
VMEM_LIMIT = 53 * 2**20 + 2**19
CUT = 8
LAST = 15
MESH = pl.DeviceIdType.MESH
HALO, COMP, RS = 1, 1, 3
f32 = jnp.float32
bf16 = jnp.bfloat16


def kernel(
    shift_ref, live_ref, psi, left, right, out,
    lbuf, rbuf, win0, win1, acc0, acc1, cex0, cex1, pair0, pair1,
    xin0, xin1, xsum0, xsum1, zin0, zin1,
    load_sem, ysend, yrecv, hsend, hrecv, esend, erecv, qsend, qrecv,
    fsend, frecv, csend, crecv, xsend, xrecv, zsend, zrecv,
):
    wins, accs, cexs, pairs = (win0, win1), (acc0, acc1), (cex0, cex1), (pair0, pair1)
    xins, xsums, zins = (xin0, xin1), (xsum0, xsum1), (zin0, zin1)
    sec, term = lax.axis_index("sec"), lax.axis_index("term")
    core = lax.rem(term, 2)
    chip = term // 2
    x = lax.rem(chip, NX)
    z = chip // NX
    xa = (lax.rem(x + NX - 1, NX), lax.rem(x + 1, NX))

    def dev(s, zz, xx, cc):
        return (s, (zz * NX + xx) * 2 + cc)

    sibling = dev(sec, z, x, 1 - core)
    xpeer = [dev(sec, z, xx, core) for xx in xa]
    xring = [dev(sec, z, lax.rem(x + k, NX), core) for k in (1, 2, 3)]
    zpeer = [dev(sec, lax.rem(z + k, NZ), x, core) for k in (1, 2, 3)]
    has = (sec > 0, sec < LAST)
    cross = (sec == CUT, sec == CUT - 1)
    direct = tuple(jnp.logical_and(h, jnp.logical_not(c)) for h, c in zip(has, cross))
    ypeer = (
        dev(sec - 1, jnp.where(cross[0], NZ - 1 - z, z), x, core),
        dev(sec + 1, jnp.where(cross[1], NZ - 1 - z, z), x, core),
    )

    loads = [
        pltpu.make_async_copy(psi.at[:, 0], win0.at[pl.ds(2, 2)], load_sem.at[0]),
        pltpu.make_async_copy(psi.at[:, 1], win1.at[pl.ds(2, 2)], load_sem.at[1]),
        pltpu.make_async_copy(left.at[0], lbuf, load_sem.at[2]),
        pltpu.make_async_copy(right.at[0], rbuf, load_sem.at[3]),
    ]
    for copy in loads:
        copy.start()

    barrier = pltpu.get_barrier_semaphore()
    for peer in [sibling] + xring + zpeer:
        pl.semaphore_signal(barrier, inc=1, device_id=peer, device_id_type=MESH)
    for side in (0, 1):
        @pl.when(has[side])
        def _():
            pl.semaphore_signal(barrier, inc=1, device_id=ypeer[side], device_id_type=MESH)

    ends = jnp.where(has[0], 1, 0) + jnp.where(has[1], 1, 0)
    pl.semaphore_wait(barrier, 7 + ends)

    def remote(src, dst, ssem, rsem, device):
        return pltpu.make_async_remote_copy(
            src_ref=src, dst_ref=dst, send_sem=ssem, recv_sem=rsem, device_id=device, device_id_type=MESH
        )

    odd = lax.rem(x, 2)

    def block_rows(n):
        return pl.ds(pl.multiple_of(n * QR, QR), QR)

    def shared_rows(parity, q):
        return pl.ds(pl.multiple_of(parity * NF + q * HF, HF), HF)

    def y_rows(side, j):
        return pl.ds(2 * NF, ND) if j == 2 else shared_rows(odd, j ^ side)

    def spot(side):
        return core + 4 * side

    def y_copy(v, side, j, landing):
        at = side if landing else 1 - side
        part = y_rows(at, j)
        return remote(
            psi.at[core, v, part], wins[v].at[spot(at), part], ysend.at[v, side, j], yrecv.at[v, at, j], ypeer[side]
        )

    def h_copy(v, side, q, landing):
        part = shared_rows(1 - odd, q) if landing else shared_rows(odd, q)
        place = wins[v].at[spot(side), part]
        return remote(place, place, hsend.at[v, side, q], hrecv.at[v, side, q], xpeer[q])

    def piece_rows(n, h):
        return pl.ds(pl.multiple_of(n * QR + h * QH, QH), QH)

    def e_copy(v, side, h, landing):
        at = side if landing else 1 - side
        part = piece_rows(x, h)
        return remote(
            psi.at[core, v, part], wins[v].at[spot(at), part], esend.at[v, side, h], erecv.at[v, at, h], ypeer[side]
        )

    def q_copy(v, side, h, k, landing):
        place = wins[v].at[spot(side), piece_rows(lax.rem(x + 3 - k, NX) if landing else x, h)]
        return remote(place, place, qsend.at[v, side, 3 * h + k], qrecv.at[v, side, 3 * h + k], xring[k])

    def pass_on(v, side, part, n):
        place = wins[v].at[spot(side), part]
        return remote(place, place, fsend.at[v, side, n], frecv.at[v, side], sibling)

    def passed(v, side):
        place = wins[v].at[1 - core + 4 * side]
        return remote(place, place, fsend.at[v, side, 0], frecv.at[v, side], sibling)

    def issue_y(v, j):
        if j == 2 and not ND:
            return
        for side in (0, 1):
            @pl.when(direct[side])
            def _():
                y_copy(v, side, j, False).start()

    def issue_e(v, h):
        for side in (0, 1):
            @pl.when(cross[side])
            def _():
                e_copy(v, side, h, False).start()

    def pass_y(v, j):
        if j == 2 and not ND:
            return
        for side in (0, 1):
            @pl.when(direct[side])
            def _():
                y_copy(v, side, j, True).wait_recv()
                if j < 2:
                    h_copy(v, side, j ^ side, False).start()
                pass_on(v, side, y_rows(side, j), j).start()

    def pass_x(v, j):
        for side in (0, 1):
            @pl.when(direct[side])
            def _():
                h_copy(v, side, j ^ side, True).wait_recv()
                pass_on(v, side, shared_rows(1 - odd, j ^ side), 3 + j).start()

    def pass_e(v, h):
        for side in (0, 1):
            @pl.when(cross[side])
            def _():
                e_copy(v, side, h, True).wait_recv()
                for k in range(3):
                    q_copy(v, side, h, k, False).start()
                if h == 1:
                    pass_on(v, side, block_rows(x), 0).start()

    def pass_q(v):
        for side in (0, 1):
            @pl.when(cross[side])
            def _():
                for k in (0, 2, 1):
                    for h in (0, 1):
                        q_copy(v, side, h, k, True).wait_recv()
                    pass_on(v, side, block_rows(lax.rem(x + 3 - k, NX)), 1 + k).start()

    def finish(v):
        for side in (0, 1):
            @pl.when(has[side])
            def _():
                passed(v, side).wait_recv()

    def drain(v):
        for side in (0, 1):
            @pl.when(direct[side])
            def _():
                for j in (0, 1, 2):
                    if j < 2 or ND:
                        y_copy(v, side, j, False).wait_send()
                        pass_on(v, side, y_rows(side, j), j).wait_send()
                for j in (0, 1):
                    h_copy(v, side, j, False).wait_send()
                    pass_on(v, side, shared_rows(0, 0), 3 + j).wait_send()

            @pl.when(cross[side])
            def _():
                for h in (0, 1):
                    e_copy(v, side, h, False).wait_send()
                    for k in range(3):
                        q_copy(v, side, h, k, False).wait_send()
                for n in range(4):
                    pass_on(v, side, block_rows(0), n).wait_send()

    def exchange(v, s):
        return remote(accs[v].at[s, :, 1 - core], cexs[v].at[s], csend.at[v, s], crecv.at[v, s], sibling)

    def xhop(v, s, k):
        return remote(
            pairs[v].at[s, :, lax.rem(x + 1 + k, NX)], xins[v].at[s, k], xsend.at[v, s, k], xrecv.at[v, s, k], xring[k]
        )

    def zhop(v, s, k):
        return remote(
            xsums[v].at[s, lax.rem(z + 1 + k, NZ)], zins[v].at[s, k], zsend.at[v, s, k], zrecv.at[v, s, k], zpeer[k]
        )

    def compute(v, s):
        block = wins[v][s + 2 - shift_ref[0]]
        inner = jnp.dot(lbuf[s], block, preferred_element_type=f32).astype(bf16)
        outer = lax.dot_general(inner, rbuf[s], (((1,), (1,)), ((), ())), preferred_element_type=f32)
        outer = outer * live_ref[0].astype(f32)
        accs[v][s] = outer.astype(bf16).reshape(NX * NZ, 2, RB, B)

    def products(v):
        for s in range(2):
            if COMP:
                compute(v, s)
            if RS >= 1:
                exchange(v, s).start()

    def add_cores(v):
        for s in range(2 if RS >= 1 else 0):
            exchange(v, s).wait_recv()
            both = accs[v][s, :, core].astype(f32) + cexs[v][s].astype(f32)
            pairs[v][s] = both.astype(bf16).reshape(NZ, NX, RB, B)
            if RS >= 2:
                for k in range(3):
                    xhop(v, s, k).start()

    def add_x(v):
        for s in range(2 if RS >= 2 else 0):
            total = pairs[v][s, :, x].astype(f32)
            for k in range(3):
                xhop(v, s, k).wait_recv()
                total += xins[v][s, k].astype(f32)
            xsums[v][s] = total.astype(bf16)
            if RS >= 3:
                for k in range(3):
                    zhop(v, s, k).start()

    def add_z(v):
        for s in range(2 if RS >= 3 else 0):
            total = xsums[v][s, z].astype(f32)
            for k in range(3):
                zhop(v, s, k).wait_recv()
                total += zins[v][s, k].astype(f32)
            out[s, v] = total.astype(bf16)

    if HALO:
        issue_y(0, 0)
        issue_e(0, 0)
        issue_y(0, 1)
        issue_e(0, 1)
        issue_y(0, 2)
    for side in (0, 1):
        @pl.when(jnp.logical_not(has[side]))
        def _():
            for v in range(V):
                for at in range(2):
                    wins[v][4 * side + at] = jnp.zeros((B, B), bf16)

    for copy in loads:
        copy.wait()

    at_cut = jnp.logical_or(cross[0], cross[1])
    if HALO:
        pass_y(0, 0)
        issue_y(1, 0)
        pass_e(0, 0)
        issue_e(1, 0)
        pass_y(0, 1)
        issue_y(1, 1)
        pass_e(0, 1)
        issue_e(1, 1)
        pass_x(0, 0)
        pass_y(0, 2)
        issue_y(1, 2)
        pass_e(1, 0)
        pass_x(0, 1)
        pass_y(1, 0)

        @pl.when(at_cut)
        def _():
            pass_e(1, 1)
            pass_y(1, 1)
            pass_q(0)

        finish(0)
    products(0)
    if HALO:
        @pl.when(jnp.logical_not(at_cut))
        def _():
            pass_y(1, 1)

    add_cores(0)
    if HALO:
        pass_x(1, 0)
        pass_y(1, 2)
        pass_x(1, 1)
        pass_q(1)
        finish(1)
    products(1)
    add_cores(1)
    add_x(0)
    add_z(0)
    add_x(1)
    add_z(1)

    for v in range(V):
        if HALO:
            drain(v)
        for s in range(2):
            if RS >= 1:
                exchange(v, s).wait_send()
            if RS >= 2:
                for k in range(3):
                    xhop(v, s, k).wait_send()
            if RS >= 3:
                for k in range(3):
                    zhop(v, s, k).wait_send()


def local(psi, left_ops, right_ops, shift, live):
    dma = pltpu.SemaphoreType.DMA
    per_vector = lambda shape: [pltpu.VMEM(shape, bf16)] * V
    hbm = pl.BlockSpec(memory_space=pltpu.HBM)
    smem = pl.BlockSpec(memory_space=pltpu.SMEM)
    return pl.pallas_call(
        kernel,
        out_shape=jax.ShapeDtypeStruct((2, V, RB, B), bf16),
        in_specs=[smem, smem, hbm, hbm, hbm],
        out_specs=pl.BlockSpec(memory_space=pltpu.VMEM),
        scratch_shapes=[pltpu.VMEM((2, B, B), bf16)] * 2
        + per_vector((6, B, B))
        + per_vector((2, NX * NZ, 2, RB, B))
        + per_vector((2, NX * NZ, RB, B))
        + per_vector((2, NZ, NX, RB, B))
        + per_vector((2, 3, NZ, RB, B))
        + per_vector((2, NZ, RB, B))
        + per_vector((2, 3, RB, B))
        + [dma((4,))]
        + [dma((V, 2, 3))] * 2
        + [dma((V, 2, 2))] * 2
        + [dma((V, 2, 2))] * 2
        + [dma((V, 2, 6))] * 2
        + [dma((V, 2, 5)), dma((V, 2))]
        + [dma((V, 2))] * 2
        + [dma((V, 2, 3))] * 4,
        compiler_params=pltpu.CompilerParams(
            collective_id=0, has_side_effects=True, vmem_limit_bytes=VMEM_LIMIT
        ),
        name="sigma",
    )(shift, live, psi, left_ops, right_ops)


def solution(mesh):
    in_specs = (
        P("sec", None, None, None),
        P("term", "sec", None, None),
        P("term", "sec", None, None),
        P("term"),
        P("term"),
    )
    out_specs = P("sec", None, "term", None)
    return jax.shard_map(local, mesh=mesh, in_specs=in_specs, out_specs=out_specs, check_vma=False)
```

```python
import jax
import jax.numpy as jnp
from jax import lax
from jax.experimental import pallas as pl
from jax.experimental.pallas import tpu as pltpu
from jax.sharding import PartitionSpec as P

B = 512
V = 2
NX = 4
NZ = 4
RB = 16
QR = B // NX
QH = QR // 2
NF = 128
HF = NF // 2
ND = B - 2 * NF
VMEM_LIMIT = 53 * 2**20 + 2**19
CUT = 8
LAST = 15
MESH = pl.DeviceIdType.MESH
f32 = jnp.float32
bf16 = jnp.bfloat16


def kernel(
    shift_ref, live_ref, psi, left, right, out,
    lbuf, rbuf, rbuf0, rbuf1, win0, win1, acc0, acc1, cex0, cex1, pair0, pair1,
    xin0, xin1, xsum0, xsum1, zin0, zin1,
    load_sem, ysend, yrecv, hsend, hrecv, esend, erecv, rsend, rrecv, qsend, qrecv,
    fsend, frecv, csend, crecv, xsend, xrecv, zsend, zrecv,
):
    wins, accs, cexs, pairs = (win0, win1), (acc0, acc1), (cex0, cex1), (pair0, pair1)
    xins, xsums, zins = (xin0, xin1), (xsum0, xsum1), (zin0, zin1)
    rbufs = (rbuf0, rbuf1)
    sec, term = lax.axis_index("sec"), lax.axis_index("term")
    core = lax.rem(term, 2)
    chip = term // 2
    x = lax.rem(chip, NX)
    z = chip // NX
    xa = (lax.rem(x + NX - 1, NX), lax.rem(x + 1, NX))

    def dev(s, zz, xx, cc):
        return (s, (zz * NX + xx) * 2 + cc)

    sibling = dev(sec, z, x, 1 - core)
    xpeer = [dev(sec, z, xx, core) for xx in xa]
    xring = [dev(sec, z, lax.rem(x + k, NX), core) for k in (1, 2, 3)]
    zpeer = [dev(sec, lax.rem(z + k, NZ), x, core) for k in (1, 2, 3)]
    has = (sec > 0, sec < LAST)
    cross = (sec == CUT, sec == CUT - 1)
    direct = tuple(jnp.logical_and(h, jnp.logical_not(c)) for h, c in zip(has, cross))
    ypeer = (
        dev(sec - 1, jnp.where(cross[0], NZ - 1 - z, z), x, core),
        dev(sec + 1, jnp.where(cross[1], NZ - 1 - z, z), x, core),
    )

    relay = (sec == LAST, sec == 0)
    y = lax.rem(sec, CUT)
    corner = jnp.logical_or(y == 0, y == CUT - 1)
    across = dev(lax.rem(sec + CUT, 2 * CUT), NZ - 1 - z, x, core)
    around = dev(sec + CUT - 1 - 2 * y, z, x, core)

    loads = [
        pltpu.make_async_copy(psi.at[:, 0], win0.at[pl.ds(2, 2)], load_sem.at[0]),
        pltpu.make_async_copy(psi.at[:, 1], win1.at[pl.ds(2, 2)], load_sem.at[1]),
        pltpu.make_async_copy(left.at[0], lbuf, load_sem.at[2]),
        pltpu.make_async_copy(right.at[0], rbuf, load_sem.at[3]),
    ]
    for copy in loads:
        copy.start()

    barrier = pltpu.get_barrier_semaphore()
    for peer in [sibling] + xring + zpeer:
        pl.semaphore_signal(barrier, inc=1, device_id=peer, device_id_type=MESH)
    for side in (0, 1):
        @pl.when(has[side])
        def _():
            pl.semaphore_signal(barrier, inc=1, device_id=ypeer[side], device_id_type=MESH)

    @pl.when(corner)
    def _():
        pl.semaphore_signal(barrier, inc=1, device_id=across, device_id_type=MESH)
        pl.semaphore_signal(barrier, inc=1, device_id=around, device_id_type=MESH)

    ends = jnp.where(has[0], 1, 0) + jnp.where(has[1], 1, 0) + jnp.where(corner, 2, 0)
    pl.semaphore_wait(barrier, 7 + ends)

    def remote(src, dst, ssem, rsem, device):
        return pltpu.make_async_remote_copy(
            src_ref=src, dst_ref=dst, send_sem=ssem, recv_sem=rsem, device_id=device, device_id_type=MESH
        )

    odd, zodd = lax.rem(x, 2), lax.rem(z, 2)
    quarter = [lax.rem(x + 2 * zodd + n, NX) for n in range(NX)]
    sharers = (xring[0], dev(sec, z + 1 - 2 * zodd, x, core), xring[2])

    def block_rows(n):
        return pl.ds(pl.multiple_of(n * QR, QR), QR)

    def shared_rows(parity, q):
        return pl.ds(pl.multiple_of(parity * NF + q * HF, HF), HF)

    def y_rows(side, j):
        return pl.ds(2 * NF, ND) if j == 2 else shared_rows(odd, j ^ side)

    def spot(side):
        return core + 4 * side

    def y_copy(v, side, j, landing):
        at = side if landing else 1 - side
        part = y_rows(at, j)
        return remote(
            psi.at[core, v, part], wins[v].at[spot(at), part], ysend.at[v, side, j], yrecv.at[v, at, j], ypeer[side]
        )

    def h_copy(v, side, q, landing):
        part = shared_rows(1 - odd, q) if landing else shared_rows(odd, q)
        place = wins[v].at[spot(side), part]
        return remote(place, place, hsend.at[v, side, q], hrecv.at[v, side, q], xpeer[q])

    def piece_rows(n, h):
        return pl.ds(pl.multiple_of(n * QR + h * QH, QH), QH)

    def e_copy(v, side, h, landing):
        at = side if landing else 1 - side
        part = piece_rows(quarter[0] if landing else quarter[2], h)
        if h == 1 and not landing:
            return remote(psi.at[core, v, part], rbufs[v], esend.at[v, side, h], rrecv.at[v], across)
        return remote(
            psi.at[core, v, part], wins[v].at[spot(at), part], esend.at[v, side, h], erecv.at[v, at, h], ypeer[side]
        )

    def r_copy(v, side):
        part = piece_rows(quarter[0], 1)
        return remote(rbufs[v], wins[v].at[spot(side), part], rsend.at[v], erecv.at[v, side, 1], around)

    def r_wait(v):
        return remote(rbufs[v], rbufs[v], rsend.at[v], rrecv.at[v], across)

    def pass_r(v):
        for side in (0, 1):
            @pl.when(relay[side])
            def _():
                r_wait(v).wait_recv()
                r_copy(v, side).start()

    def q_copy(v, side, h, k, landing):
        place = wins[v].at[spot(side), piece_rows(quarter[3 - k if landing else 0], h)]
        return remote(place, place, qsend.at[v, side, 3 * h + k], qrecv.at[v, side, 3 * h + k], sharers[k])

    def pass_on(v, side, part, n):
        place = wins[v].at[spot(side), part]
        return remote(place, place, fsend.at[v, side, n], frecv.at[v, side], sibling)

    def passed(v, side):
        place = wins[v].at[1 - core + 4 * side]
        return remote(place, place, fsend.at[v, side, 0], frecv.at[v, side], sibling)

    def issue_y(v, j):
        for side in (0, 1):
            @pl.when(direct[side])
            def _():
                y_copy(v, side, j, False).start()

    def issue_e(v, h):
        for side in (0, 1):
            @pl.when(cross[side])
            def _():
                e_copy(v, side, h, False).start()

    def pass_y(v, j):
        for side in (0, 1):
            @pl.when(direct[side])
            def _():
                y_copy(v, side, j, True).wait_recv()
                if j < 2:
                    h_copy(v, side, j ^ side, False).start()
                pass_on(v, side, y_rows(side, j), j).start()

    def pass_x(v, j):
        for side in (0, 1):
            @pl.when(direct[side])
            def _():
                h_copy(v, side, j ^ side, True).wait_recv()
                pass_on(v, side, shared_rows(1 - odd, j ^ side), 3 + j).start()

    def pass_e(v, h):
        for side in (0, 1):
            @pl.when(cross[side])
            def _():
                e_copy(v, side, h, True).wait_recv()
                for k in range(3):
                    q_copy(v, side, h, k, False).start()
                if h == 1:
                    pass_on(v, side, block_rows(quarter[0]), 0).start()

    def pass_q(v):
        for side in (0, 1):
            @pl.when(cross[side])
            def _():
                for k in (0, 2, 1):
                    for h in (0, 1):
                        q_copy(v, side, h, k, True).wait_recv()
                    pass_on(v, side, block_rows(quarter[3 - k]), 1 + k).start()

    def finish(v):
        for side in (0, 1):
            @pl.when(has[side])
            def _():
                passed(v, side).wait_recv()

    def drain(v):
        for side in (0, 1):
            @pl.when(direct[side])
            def _():
                for j in (0, 1, 2):
                    if True:
                        y_copy(v, side, j, False).wait_send()
                        pass_on(v, side, y_rows(side, j), j).wait_send()
                for j in (0, 1):
                    h_copy(v, side, j, False).wait_send()
                    pass_on(v, side, shared_rows(0, 0), 3 + j).wait_send()

            @pl.when(relay[side])
            def _():
                r_copy(v, side).wait_send()

            @pl.when(cross[side])
            def _():
                for h in (0, 1):
                    e_copy(v, side, h, False).wait_send()
                    for k in range(3):
                        q_copy(v, side, h, k, False).wait_send()
                for n in range(4):
                    pass_on(v, side, block_rows(0), n).wait_send()

    def exchange(v, s):
        return remote(accs[v].at[s, :, 1 - core], cexs[v].at[s], csend.at[v, s], crecv.at[v, s], sibling)

    def xhop(v, s, k):
        return remote(
            pairs[v].at[s, :, lax.rem(x + 1 + k, NX)], xins[v].at[s, k], xsend.at[v, s, k], xrecv.at[v, s, k], xring[k]
        )

    def zhop(v, s, k):
        return remote(
            xsums[v].at[s, lax.rem(z + 1 + k, NZ)], zins[v].at[s, k], zsend.at[v, s, k], zrecv.at[v, s, k], zpeer[k]
        )

    def compute(v, s):
        block = wins[v][s + 2 - shift_ref[0]]
        inner = jnp.dot(lbuf[s], block, preferred_element_type=f32).astype(bf16)
        outer = lax.dot_general(inner, rbuf[s], (((1,), (1,)), ((), ())), preferred_element_type=f32)
        outer = outer * live_ref[0].astype(f32)
        accs[v][s] = outer.astype(bf16).reshape(NX * NZ, 2, RB, B)

    def products(v):
        for s in range(2):
            compute(v, s)
            exchange(v, s).start()

    def add_cores(v):
        for s in range(2):
            exchange(v, s).wait_recv()
            both = accs[v][s, :, core].astype(f32) + cexs[v][s].astype(f32)
            pairs[v][s] = both.astype(bf16).reshape(NZ, NX, RB, B)
            for k in (1, 0, 2):
                xhop(v, s, k).start()

    def add_x(v):
        for s in range(2):
            total = pairs[v][s, :, x].astype(f32)
            for k in range(3):
                xhop(v, s, k).wait_recv()
                total += xins[v][s, k].astype(f32)
            xsums[v][s] = total.astype(bf16)
            for k in range(3):
                zhop(v, s, k).start()

    def add_z(v):
        for s in range(2):
            total = xsums[v][s, z].astype(f32)
            for k in range(3):
                zhop(v, s, k).wait_recv()
                total += zins[v][s, k].astype(f32)
            out[s, v] = total.astype(bf16)

    issue_y(0, 0)
    for v in range(V):
        for h in (0, 1):
            issue_e(v, h)
    issue_y(0, 1)
    issue_y(0, 2)
    for side in (0, 1):
        @pl.when(jnp.logical_not(has[side]))
        def _():
            for v in range(V):
                for at in range(2):
                    wins[v][4 * side + at] = jnp.zeros((B, B), bf16)

    for copy in loads:
        copy.wait()

    at_cut = jnp.logical_or(cross[0], cross[1])
    pass_y(0, 0)
    issue_y(1, 0)
    pass_y(0, 1)
    issue_y(1, 1)
    pass_r(0)
    pass_e(0, 0)
    pass_x(0, 0)
    pass_x(0, 1)
    pass_r(1)
    pass_e(1, 0)
    pass_e(0, 1)
    pass_y(0, 2)
    issue_y(1, 2)
    pass_y(1, 0)

    @pl.when(at_cut)
    def _():
        pass_e(1, 1)
        pass_y(1, 1)
        pass_q(0)

    finish(0)
    products(0)
    @pl.when(jnp.logical_not(at_cut))
    def _():
        pass_y(1, 1)

    add_cores(0)
    pass_x(1, 0)
    pass_y(1, 2)
    pass_x(1, 1)
    pass_q(1)
    finish(1)
    products(1)
    add_cores(1)
    add_x(0)
    add_z(0)
    add_x(1)
    add_z(1)

    for v in range(V):
        drain(v)
        for s in range(2):
            exchange(v, s).wait_send()
            for k in range(3):
                xhop(v, s, k).wait_send()
            for k in range(3):
                zhop(v, s, k).wait_send()


def local(psi, left_ops, right_ops, shift, live):
    dma = pltpu.SemaphoreType.DMA
    per_vector = lambda shape: [pltpu.VMEM(shape, bf16)] * V
    hbm = pl.BlockSpec(memory_space=pltpu.HBM)
    smem = pl.BlockSpec(memory_space=pltpu.SMEM)
    return pl.pallas_call(
        kernel,
        out_shape=jax.ShapeDtypeStruct((2, V, RB, B), bf16),
        in_specs=[smem, smem, hbm, hbm, hbm],
        out_specs=pl.BlockSpec(memory_space=pltpu.VMEM),
        scratch_shapes=[pltpu.VMEM((2, B, B), bf16)] * 2
        + per_vector((QH, B))
        + per_vector((6, B, B))
        + per_vector((2, NX * NZ, 2, RB, B))
        + per_vector((2, NX * NZ, RB, B))
        + per_vector((2, NZ, NX, RB, B))
        + per_vector((2, 3, NZ, RB, B))
        + per_vector((2, NZ, RB, B))
        + per_vector((2, 3, RB, B))
        + [dma((4,))]
        + [dma((V, 2, 3))] * 2
        + [dma((V, 2, 2))] * 2
        + [dma((V, 2, 2))] * 2
        + [dma((V,))] * 2
        + [dma((V, 2, 6))] * 2
        + [dma((V, 2, 5)), dma((V, 2))]
        + [dma((V, 2))] * 2
        + [dma((V, 2, 3))] * 4,
        compiler_params=pltpu.CompilerParams(
            collective_id=0, has_side_effects=True, vmem_limit_bytes=VMEM_LIMIT
        ),
        name="sigma",
    )(shift, live, psi, left_ops, right_ops)


def solution(mesh):
    in_specs = (
        P("sec", None, None, None),
        P("term", "sec", None, None),
        P("term", "sec", None, None),
        P("term"),
        P("term"),
    )
    out_specs = P("sec", None, "term", None)
    return jax.shard_map(local, mesh=mesh, in_specs=in_specs, out_specs=out_specs, check_vma=False)
```

```python
import jax
import jax.numpy as jnp
from jax import lax
from jax.experimental import pallas as pl
from jax.experimental.pallas import tpu as pltpu
from jax.sharding import PartitionSpec as P

B = 512
V = 2
NX = 4
NZ = 4
RB = 16
QR = B // NX
QH = QR // 2
NF = 128
HF = NF // 2
ND = B - 2 * NF
VMEM_LIMIT = 53 * 2**20 + 2**19
CUT = 8
LAST = 15
MESH = pl.DeviceIdType.MESH
f32 = jnp.float32
bf16 = jnp.bfloat16


def kernel(
    shift_ref, live_ref, psi, left, right, out,
    lbuf, rbuf, rbuf0, rbuf1, win0, win1, acc0, acc1, cex0, cex1, pair0, pair1,
    xin0, xin1, xsum0, xsum1, zin0, zin1,
    load_sem, ysend, yrecv, hsend, hrecv, esend, erecv, rsend, rrecv, qsend, qrecv,
    fsend, frecv, csend, crecv, xsend, xrecv, zsend, zrecv,
):
    wins, accs, cexs, pairs = (win0, win1), (acc0, acc1), (cex0, cex1), (pair0, pair1)
    xins, xsums, zins = (xin0, xin1), (xsum0, xsum1), (zin0, zin1)
    rbufs = (rbuf0, rbuf1)
    sec, term = lax.axis_index("sec"), lax.axis_index("term")
    core = lax.rem(term, 2)
    chip = term // 2
    x = lax.rem(chip, NX)
    z = chip // NX
    xa = (lax.rem(x + NX - 1, NX), lax.rem(x + 1, NX))

    def dev(s, zz, xx, cc):
        return (s, (zz * NX + xx) * 2 + cc)

    sibling = dev(sec, z, x, 1 - core)
    xpeer = [dev(sec, z, xx, core) for xx in xa]
    xring = [dev(sec, z, lax.rem(x + k, NX), core) for k in (1, 2, 3)]
    zpeer = [dev(sec, lax.rem(z + k, NZ), x, core) for k in (1, 2, 3)]
    has = (sec > 0, sec < LAST)
    cross = (sec == CUT, sec == CUT - 1)
    direct = tuple(jnp.logical_and(h, jnp.logical_not(c)) for h, c in zip(has, cross))
    ypeer = (
        dev(sec - 1, jnp.where(cross[0], NZ - 1 - z, z), x, core),
        dev(sec + 1, jnp.where(cross[1], NZ - 1 - z, z), x, core),
    )

    relay = (sec == LAST, sec == 0)
    y = lax.rem(sec, CUT)
    corner = jnp.logical_or(y == 0, y == CUT - 1)
    across = dev(lax.rem(sec + CUT, 2 * CUT), NZ - 1 - z, x, core)
    around = dev(sec + CUT - 1 - 2 * y, z, x, core)

    loads = [
        pltpu.make_async_copy(psi.at[:, 0], win0.at[pl.ds(2, 2)], load_sem.at[0]),
        pltpu.make_async_copy(psi.at[:, 1], win1.at[pl.ds(2, 2)], load_sem.at[1]),
        pltpu.make_async_copy(left.at[0], lbuf, load_sem.at[2]),
        pltpu.make_async_copy(right.at[0], rbuf, load_sem.at[3]),
    ]
    for copy in loads:
        copy.start()

    barrier = pltpu.get_barrier_semaphore()
    for peer in [sibling] + xring + zpeer:
        pl.semaphore_signal(barrier, inc=1, device_id=peer, device_id_type=MESH)
    for side in (0, 1):
        @pl.when(has[side])
        def _():
            pl.semaphore_signal(barrier, inc=1, device_id=ypeer[side], device_id_type=MESH)

    @pl.when(corner)
    def _():
        pl.semaphore_signal(barrier, inc=1, device_id=across, device_id_type=MESH)
        pl.semaphore_signal(barrier, inc=1, device_id=around, device_id_type=MESH)

    ends = jnp.where(has[0], 1, 0) + jnp.where(has[1], 1, 0) + jnp.where(corner, 2, 0)
    pl.semaphore_wait(barrier, 7 + ends)

    def remote(src, dst, ssem, rsem, device):
        return pltpu.make_async_remote_copy(
            src_ref=src, dst_ref=dst, send_sem=ssem, recv_sem=rsem, device_id=device, device_id_type=MESH
        )

    odd, zodd = lax.rem(x, 2), lax.rem(z, 2)
    quarter = [lax.rem(x + 2 * zodd + n, NX) for n in range(NX)]
    sharers = (xring[0], dev(sec, z + 1 - 2 * zodd, x, core), xring[2])

    def block_rows(n):
        return pl.ds(pl.multiple_of(n * QR, QR), QR)

    def shared_rows(parity, q):
        return pl.ds(pl.multiple_of(parity * NF + q * HF, HF), HF)

    def y_rows(side, j):
        return pl.ds(2 * NF, ND) if j == 2 else shared_rows(odd, j ^ side)

    def spot(side):
        return core + 4 * side

    def y_copy(v, side, j, landing):
        at = side if landing else 1 - side
        part = y_rows(at, j)
        return remote(
            psi.at[core, v, part], wins[v].at[spot(at), part], ysend.at[v, side, j], yrecv.at[v, at, j], ypeer[side]
        )

    def h_copy(v, side, q, landing):
        part = shared_rows(1 - odd, q) if landing else shared_rows(odd, q)
        place = wins[v].at[spot(side), part]
        return remote(place, place, hsend.at[v, side, q], hrecv.at[v, side, q], xpeer[q])

    def piece_rows(n, h):
        return pl.ds(pl.multiple_of(n * QR + h * QH, QH), QH)

    def e_copy(v, side, h, landing):
        at = side if landing else 1 - side
        part = piece_rows(quarter[0] if landing else quarter[2], h)
        if h == 1 and not landing:
            return remote(psi.at[core, v, part], rbufs[v], esend.at[v, side, h], rrecv.at[v], across)
        return remote(
            psi.at[core, v, part], wins[v].at[spot(at), part], esend.at[v, side, h], erecv.at[v, at, h], ypeer[side]
        )

    def r_copy(v, side):
        part = piece_rows(quarter[0], 1)
        return remote(rbufs[v], wins[v].at[spot(side), part], rsend.at[v], erecv.at[v, side, 1], around)

    def r_wait(v):
        return remote(rbufs[v], rbufs[v], rsend.at[v], rrecv.at[v], across)

    def pass_r(v):
        for side in (0, 1):
            @pl.when(relay[side])
            def _():
                r_wait(v).wait_recv()
                r_copy(v, side).start()

    def q_copy(v, side, h, k, landing):
        place = wins[v].at[spot(side), piece_rows(quarter[3 - k if landing else 0], h)]
        return remote(place, place, qsend.at[v, side, 3 * h + k], qrecv.at[v, side, 3 * h + k], sharers[k])

    def pass_on(v, side, part, n):
        place = wins[v].at[spot(side), part]
        return remote(place, place, fsend.at[v, side, n], frecv.at[v, side], sibling)

    def passed(v, side):
        place = wins[v].at[1 - core + 4 * side]
        return remote(place, place, fsend.at[v, side, 0], frecv.at[v, side], sibling)

    def issue_y(v, j):
        for side in (0, 1):
            @pl.when(direct[side])
            def _():
                y_copy(v, side, j, False).start()

    def issue_e(v, h):
        for side in (0, 1):
            @pl.when(cross[side])
            def _():
                e_copy(v, side, h, False).start()

    def pass_y(v, j):
        for side in (0, 1):
            @pl.when(direct[side])
            def _():
                y_copy(v, side, j, True).wait_recv()
                if j < 2:
                    h_copy(v, side, j ^ side, False).start()
                pass_on(v, side, y_rows(side, j), j).start()

    def pass_x(v, j):
        for side in (0, 1):
            @pl.when(direct[side])
            def _():
                h_copy(v, side, j ^ side, True).wait_recv()
                pass_on(v, side, shared_rows(1 - odd, j ^ side), 3 + j).start()

    def pass_e(v, h):
        for side in (0, 1):
            @pl.when(cross[side])
            def _():
                e_copy(v, side, h, True).wait_recv()
                for k in range(3):
                    q_copy(v, side, h, k, False).start()
                if h == 1:
                    pass_on(v, side, block_rows(quarter[0]), 0).start()

    def pass_q(v):
        for side in (0, 1):
            @pl.when(cross[side])
            def _():
                for k in (0, 2, 1):
                    for h in (0, 1):
                        q_copy(v, side, h, k, True).wait_recv()
                    pass_on(v, side, block_rows(quarter[3 - k]), 1 + k).start()

    def finish(v):
        for side in (0, 1):
            @pl.when(has[side])
            def _():
                passed(v, side).wait_recv()

    def drain(v):
        for side in (0, 1):
            @pl.when(direct[side])
            def _():
                for j in (0, 1, 2):
                    if True:
                        y_copy(v, side, j, False).wait_send()
                        pass_on(v, side, y_rows(side, j), j).wait_send()
                for j in (0, 1):
                    h_copy(v, side, j, False).wait_send()
                    pass_on(v, side, shared_rows(0, 0), 3 + j).wait_send()

            @pl.when(relay[side])
            def _():
                r_copy(v, side).wait_send()

            @pl.when(cross[side])
            def _():
                for h in (0, 1):
                    e_copy(v, side, h, False).wait_send()
                    for k in range(3):
                        q_copy(v, side, h, k, False).wait_send()
                for n in range(4):
                    pass_on(v, side, block_rows(0), n).wait_send()

    def exchange(v, s):
        return remote(accs[v].at[s, :, 1 - core], cexs[v].at[s], csend.at[v, s], crecv.at[v, s], sibling)

    def xhop(v, s, k):
        return remote(
            pairs[v].at[s, :, lax.rem(x + 1 + k, NX)], xins[v].at[s, k], xsend.at[v, s, k], xrecv.at[v, s, k], xring[k]
        )

    def zhop(v, s, k):
        return remote(
            xsums[v].at[s, lax.rem(z + 1 + k, NZ)], zins[v].at[s, k], zsend.at[v, s, k], zrecv.at[v, s, k], zpeer[k]
        )

    def compute(v, s):
        block = wins[v][s + 2 - shift_ref[0]]
        inner = jnp.dot(lbuf[s], block, preferred_element_type=f32).astype(bf16)
        outer = lax.dot_general(inner, rbuf[s], (((1,), (1,)), ((), ())), preferred_element_type=f32)
        outer = outer * live_ref[0].astype(f32)
        accs[v][s] = outer.astype(bf16).reshape(NX * NZ, 2, RB, B)

    def products(v):
        for s in range(2):
            compute(v, s)
            exchange(v, s).start()

    def add_cores(v):
        for s in range(2):
            exchange(v, s).wait_recv()
            both = accs[v][s, :, core].astype(f32) + cexs[v][s].astype(f32)
            pairs[v][s] = both.astype(bf16).reshape(NZ, NX, RB, B)
            for k in (1, 0, 2):
                xhop(v, s, k).start()

    def add_x(v):
        for s in range(2):
            total = pairs[v][s, :, x].astype(f32)
            for k in range(3):
                xhop(v, s, k).wait_recv()
                total += xins[v][s, k].astype(f32)
            xsums[v][s] = total.astype(bf16)
            for k in range(3):
                zhop(v, s, k).start()

    def add_z(v):
        for s in range(2):
            total = xsums[v][s, z].astype(f32)
            for k in range(3):
                zhop(v, s, k).wait_recv()
                total += zins[v][s, k].astype(f32)
            out[s, v] = total.astype(bf16)

    issue_y(0, 0)
    for v in range(V):
        for h in (0, 1):
            issue_e(v, h)
    issue_y(0, 1)
    issue_y(0, 2)
    for side in (0, 1):
        @pl.when(jnp.logical_not(has[side]))
        def _():
            for v in range(V):
                for at in range(2):
                    wins[v][4 * side + at] = jnp.zeros((B, B), bf16)

    for copy in loads:
        copy.wait()

    at_cut = jnp.logical_or(cross[0], cross[1])
    pass_y(0, 0)
    issue_y(1, 0)
    pass_y(0, 1)
    issue_y(1, 1)
    pass_r(0)
    pass_e(0, 0)
    pass_x(0, 0)
    pass_x(0, 1)
    pass_r(1)
    pass_e(1, 0)
    pass_e(0, 1)
    pass_y(0, 2)
    issue_y(1, 2)
    pass_y(1, 0)

    @pl.when(at_cut)
    def _():
        pass_e(1, 1)
        pass_y(1, 1)
        pass_q(0)

    finish(0)
    products(0)
    @pl.when(jnp.logical_not(at_cut))
    def _():
        pass_y(1, 1)

    add_cores(0)
    pass_x(1, 0)
    pass_x(1, 1)
    pass_q(1)
    pass_y(1, 2)
    finish(1)
    products(1)
    add_cores(1)
    add_x(0)
    add_z(0)
    add_x(1)
    add_z(1)

    for v in range(V):
        drain(v)
        for s in range(2):
            exchange(v, s).wait_send()
            for k in range(3):
                xhop(v, s, k).wait_send()
            for k in range(3):
                zhop(v, s, k).wait_send()


def local(psi, left_ops, right_ops, shift, live):
    dma = pltpu.SemaphoreType.DMA
    per_vector = lambda shape: [pltpu.VMEM(shape, bf16)] * V
    hbm = pl.BlockSpec(memory_space=pltpu.HBM)
    smem = pl.BlockSpec(memory_space=pltpu.SMEM)
    return pl.pallas_call(
        kernel,
        out_shape=jax.ShapeDtypeStruct((2, V, RB, B), bf16),
        in_specs=[smem, smem, hbm, hbm, hbm],
        out_specs=pl.BlockSpec(memory_space=pltpu.VMEM),
        scratch_shapes=[pltpu.VMEM((2, B, B), bf16)] * 2
        + per_vector((QH, B))
        + per_vector((6, B, B))
        + per_vector((2, NX * NZ, 2, RB, B))
        + per_vector((2, NX * NZ, RB, B))
        + per_vector((2, NZ, NX, RB, B))
        + per_vector((2, 3, NZ, RB, B))
        + per_vector((2, NZ, RB, B))
        + per_vector((2, 3, RB, B))
        + [dma((4,))]
        + [dma((V, 2, 3))] * 2
        + [dma((V, 2, 2))] * 2
        + [dma((V, 2, 2))] * 2
        + [dma((V,))] * 2
        + [dma((V, 2, 6))] * 2
        + [dma((V, 2, 5)), dma((V, 2))]
        + [dma((V, 2))] * 2
        + [dma((V, 2, 3))] * 4,
        compiler_params=pltpu.CompilerParams(
            collective_id=0, has_side_effects=True, vmem_limit_bytes=VMEM_LIMIT
        ),
        name="sigma",
    )(shift, live, psi, left_ops, right_ops)


def solution(mesh):
    in_specs = (
        P("sec", None, None, None),
        P("term", "sec", None, None),
        P("term", "sec", None, None),
        P("term"),
        P("term"),
    )
    out_specs = P("sec", None, "term", None)
    return jax.shard_map(local, mesh=mesh, in_specs=in_specs, out_specs=out_specs, check_vma=False)
```
